32 devices in a mesh: req: 4 (over y, x), mlp: 8 (over z, core).
Axes of the slice: x: 2, y: 2, z: 4, core: 2. Of those that a mesh axis runs over, the one named last changes fastest.
Arguments:
- tokens: bfloat16 [64, 4608], P(('req', 'mlp')), may hold values from -6 to 6
- segments: int32 [4, 16], replicated, may hold values from 0 to 3, never falling along the last dimension, each value on 1 to 8 neighbouring positions
- owners: int32 [4], replicated, may hold values from 0 to 3, each once
- sink_keys: bfloat16 [4, 2048], P(None, 'mlp'), may hold values from -21 to 21
- sink_values: bfloat16 [4, 2048], P(None, 'mlp'), may hold values from -6 to 6
- window_keys: bfloat16 [4096, 2048], P('req', 'mlp'), may hold values from -6 to 6
- window_values: bfloat16 [4096, 2048], P('req', 'mlp'), may hold values from -6 to 6
- attn_gain: float32 [4608], replicated, may hold values from 0.1 to 1.9
- post_attn_gain: float32 [4608], replicated, may hold values from 0.1 to 1.9
- ffn_gain: float32 [4608], replicated, may hold values from 0.1 to 1.9
- post_ffn_gain: float32 [4608], replicated, may hold values from 0.1 to 1.9
- w_query: bfloat16 [4608, 4096], P(None, 'mlp'), may hold values from -0.09375 to 0.09375
- w_key: bfloat16 [4608, 2048], P(None, 'mlp'), may hold values from -0.25 to 0.25
- w_value: bfloat16 [4608, 2048], P(None, 'mlp'), may hold values from -0.09375 to 0.09375
- w_out: bfloat16 [4096, 4608], P('mlp'), may hold values from -0.09375 to 0.09375
- w_gate: bfloat16 [36864, 4608], P(('req', 'mlp')), may hold values from -0.09375 to 0.09375
- w_up: bfloat16 [36864, 4608], P(('req', 'mlp')), may hold values from -0.09375 to 0.09375
- w_down: bfloat16 [36864, 4608], P(('req', 'mlp')), may hold values from -0.03125 to 0.03125
Outputs:
- mixed: bfloat16 [64, 4608], P(('req', 'mlp'))
The draws below stay inside these ranges and needn't reach their ends.
Inputs may be any that keep to these rules, and one draw needn't show every extreme that they name: `segments`: row g gives, for the 16 suffix tokens of request group g in order, which of the group's 4 requests each belongs to; a request's tokens are contiguous and its number never falls along the row. Req index d holds array rows d * B to d * B + B - 1 of window_keys and window_values, whose window positions are owners[d] * B to owners[d] * B + B - 1, B = 4096 / 4; every block of positions is held once.
All inputs are finite; a program needn't handle non-finite values.
Results may differ from the reference program's by a relative error of at most 0.015.
Values may be sent and summed in bfloat16 or wider, within the bound.
A program may use at most 128 MiB of HBM per device.

```python
import math
import jax
import jax.numpy as jnp
import numpy as np
from jax import lax

D = 4608
HEADS = 32
KVH = 16
HD = 128
FF = 36864
WIN = 4096
SINK = 4
REQ_GRP = 4
GTOK = 16
TOKENS = 64
N_REQ = 4


def block_scale(stream_key, extent, cuts, low, largest):
    level, own = 1.0, jax.random.fold_in(stream_key, 6)
    for position, parts in cuts:
        draws = jnp.exp(jax.random.uniform(jax.random.fold_in(own, position), (parts,), jnp.float32, low / len(cuts), largest / len(cuts)))
        level = level * jnp.repeat(draws, extent[position] // parts).reshape([-1 if axis == position else 1 for axis in range(len(extent))])
    return level


def split_up(number_of, total, bound, slope):
    weights = [(1 << 20) // math.isqrt(standing ** slope) + 1 for standing in range(2, number_of + 1)]
    spare, holding = total - bound - (number_of - 1), [1] * (number_of - 1)
    while spare > 0:
        movable = [i for i in range(number_of - 1) if holding[i] < bound]
        whole, left = sum([weights[i] for i in movable]), spare
        for i in movable:
            extra = min(bound - holding[i], max(1, left * weights[i] // whole), spare)
            holding[i] = holding[i] + extra
            spare = spare - extra
    return np.array([bound] + holding)


def ragged_sizes(key, count, total, most, skew):
    if count == 2:
        one = jax.random.randint(key, (), max(1, total - most), min(most, total - 1) + 1)
        return jnp.stack([one, total - one])
    tallies = jnp.asarray(split_up(count, total, most, skew), jnp.int32)
    pairs = (count - 1) // 2
    source_of, sink = tallies[1:1 + 2 * pairs:2], tallies[2:2 + 2 * pairs:2]
    margin = jnp.minimum(source_of - 1, most - sink)
    shifted = jax.random.randint(jax.random.fold_in(key, 1), (pairs,), 0, 1 << 20) % (margin + 1)
    tallies = tallies.at[1:1 + 2 * pairs:2].set(source_of - shifted).at[2:2 + 2 * pairs:2].set(sink + shifted)
    return tallies[jax.random.permutation(jax.random.fold_in(key, 2), count)]


def centred(own_key, extent, width, reach, cuts=(), held_as=jnp.bfloat16):
    values = jax.random.normal(own_key, extent, jnp.float32) * width
    if len(cuts) > 0:
        values = block_scale(own_key, extent, cuts, -0.22, 0.18) * values
    return jnp.clip(values, min=-reach, max=reach).astype(held_as)


def setup_inputs(seed: int = 0) -> dict:
    seeds = jax.random.split(jax.random.key(seed), 19)
    tokens = centred(seeds[0], (TOKENS, D), 1.0, 6.0, ((0, 32),))
    segments = jax.vmap(lambda own: jnp.searchsorted(jnp.cumsum(ragged_sizes(own, REQ_GRP, GTOK, GTOK // 2, 2)), jnp.arange(GTOK), side="right"))(jax.random.split(seeds[1], N_REQ)).reshape((N_REQ, GTOK)).astype(jnp.int32)
    owners = jax.random.permutation(seeds[2], N_REQ).astype(jnp.int32)
    sink_keys = centred(seeds[3], (SINK, KVH * HD), 3.5, 21.0, ((1, 8),))
    sink_values = centred(seeds[4], (SINK, KVH * HD), 1.0, 6.0, ((1, 8),))
    window_keys = centred(seeds[5], (WIN, KVH * HD), 1.0, 6.0, ((0, 4), (1, 8)))
    window_values = centred(seeds[6], (WIN, KVH * HD), 1.0, 6.0, ((0, 4), (1, 8)))
    attn_gain = jnp.clip(1.0 + 0.18 * jax.random.normal(seeds[7], (D,), jnp.float32), 0.1, 1.9)
    post_attn_gain = jnp.clip(1.0 + 0.18 * jax.random.normal(seeds[8], (D,), jnp.float32), 0.1, 1.9)
    ffn_gain = jnp.clip(1.0 + 0.18 * jax.random.normal(seeds[9], (D,), jnp.float32), 0.1, 1.9)
    post_ffn_gain = jnp.clip(1.0 + 0.18 * jax.random.normal(seeds[10], (D,), jnp.float32), 0.1, 1.9)
    w_query = centred(seeds[11], (D, HEADS * HD), D ** -0.5, 0.09375, ((1, 8),))
    w_key = centred(seeds[12], (D, KVH * HD), (D // 9) ** -0.5, 0.25, ((1, 8),))
    w_value = centred(seeds[13], (D, KVH * HD), D ** -0.5, 0.09375, ((1, 8),))
    w_out = centred(seeds[14], (HEADS * HD, D), (HEADS * HD) ** -0.5, 0.09375, ((0, 8),))
    w_gate = centred(seeds[15], (FF, D), D ** -0.5, 0.09375, ((0, 32),))
    w_up = centred(seeds[16], (FF, D), D ** -0.5, 0.09375, ((0, 32),))
    w_down = centred(seeds[17], (FF, D), FF ** -0.5, 0.03125, ((0, 32),))
    return dict(tokens=tokens, segments=segments, owners=owners, sink_keys=sink_keys, sink_values=sink_values, window_keys=window_keys, window_values=window_values, attn_gain=attn_gain, post_attn_gain=post_attn_gain, ffn_gain=ffn_gain, post_ffn_gain=post_ffn_gain, w_query=w_query, w_key=w_key, w_value=w_value, w_out=w_out, w_gate=w_gate, w_up=w_up, w_down=w_down)


epsilon = 1e-06
soft_cap = 50.0
logit_scale = 1.0 / 12.0

def rms_scale(values):
    return values * lax.rsqrt(lax.optimization_barrier(jnp.mean(values * values, axis=-1, keepdims=True)) + epsilon)

def positions(seg_rows):
    ordering = jnp.arange(seg_rows.shape[-1], dtype=jnp.int32)
    same_seg = seg_rows[..., :, None] == seg_rows[..., None, :]
    earlier = ordering[None, :] < ordering[:, None]
    return lax.optimization_barrier(jnp.sum((same_seg & earlier).astype(jnp.int32), axis=-1)).astype(jnp.int32)

def attend(query_rows, key_matrix_rows, value_matrix_rows, visible):
    score_matrix = jnp.einsum('woji,roi->wojr', query_rows.astype(jnp.float32), key_matrix_rows.astype(jnp.float32)) * logit_scale
    weight = jnp.exp(soft_cap * jnp.tanh(score_matrix / soft_cap))
    weight = jnp.where(visible[:, None, None, :], weight, jnp.zeros_like(weight))
    totals = lax.optimization_barrier(jnp.sum(weight, axis=-1))
    rounded_output = lax.optimization_barrier(weight.astype(jnp.bfloat16)).astype(jnp.float32)
    summed_output = jnp.einsum('xfka,afq->xfkq', rounded_output, value_matrix_rows.astype(jnp.float32))
    return (summed_output, totals)

def reference(tokens, segments, owners, sink_keys, sink_values, window_keys, window_values, attn_gain, post_attn_gain, ffn_gain, post_ffn_gain, w_query, w_key, w_value, w_out, w_gate, w_up, w_down):
    per_kv = HEADS // KVH
    block_rows = WIN // N_REQ
    row_ids = jnp.arange(WIN, dtype=jnp.int32)
    window_pos = (owners[row_ids // block_rows] * block_rows + row_ids % block_rows).astype(jnp.int32)
    window_key = window_keys.reshape(WIN, KVH, HD)
    window_value = window_values.reshape(WIN, KVH, HD)
    sink_key = sink_keys.reshape(SINK, KVH, HD)
    sink_value = sink_values.reshape(SINK, KVH, HD)
    pos_all = positions(segments)
    token_float = tokens.astype(jnp.float32)
    normed = (rms_scale(token_float) * attn_gain).astype(jnp.bfloat16)
    ordering = jnp.arange(GTOK, dtype=jnp.int32)

    def one_group(group_index):
        group_rows = lax.dynamic_slice_in_dim(normed, (group_index * GTOK).astype(jnp.int32), GTOK, 0)
        query_rows = jnp.dot(group_rows, w_query, preferred_element_type=jnp.float32).astype(jnp.bfloat16).reshape(GTOK, KVH, per_kv, HD)
        key_new = jnp.dot(group_rows, w_key, preferred_element_type=jnp.float32).astype(jnp.bfloat16).reshape(GTOK, KVH, HD)
        value_new = jnp.dot(group_rows, w_value, preferred_element_type=jnp.float32).astype(jnp.bfloat16).reshape(GTOK, KVH, HD)
        seg_row = lax.dynamic_index_in_dim(segments, group_index, 0, keepdims=False)
        pos_row = lax.dynamic_index_in_dim(pos_all, group_index, 0, keepdims=False)
        sink_sum, sink_tot = attend(query_rows, sink_key, sink_value, jnp.ones((GTOK, SINK), dtype=jnp.bool_))
        win_sum, win_tot = attend(query_rows, window_key, window_value, window_pos[None, :] > pos_row[:, None])
        local_vis = (seg_row[:, None] == seg_row[None, :]) & (ordering[None, :] <= ordering[:, None])
        loc_sum, loc_tot = attend(query_rows, key_new, value_new, local_vis)
        merged = (sink_sum + win_sum + loc_sum) / (sink_tot + win_tot + loc_tot)[..., None]
        return merged.astype(jnp.bfloat16).reshape(GTOK, HEADS * HD)
    attended = lax.map(one_group, jnp.arange(N_REQ, dtype=jnp.int32)).reshape(TOKENS, HEADS * HD)
    projected = jnp.dot(attended, w_out, preferred_element_type=jnp.float32)
    residual = token_float + rms_scale(projected) * post_attn_gain
    ffn_in = (rms_scale(residual) * ffn_gain).astype(jnp.bfloat16)
    contract = (((1,), (1,)), ((), ()))
    gate_part = lax.dot_general(ffn_in, w_gate, contract, preferred_element_type=jnp.float32)
    up_part = lax.dot_general(ffn_in, w_up, contract, preferred_element_type=jnp.float32)
    hidden = (jax.nn.gelu(gate_part, approximate=True) * up_part).astype(jnp.bfloat16)
    ffn_out = jnp.dot(hidden, w_down, preferred_element_type=jnp.float32)
    return (residual + rms_scale(ffn_out) * post_ffn_gain).astype(jnp.bfloat16)
```

```python
import functools
import math

import jax
import jax.numpy as jnp
from jax import lax
from jax.experimental import pallas as pl
from jax.experimental.pallas import tpu as pltpu
from jax.sharding import PartitionSpec as P

HD = 128
EPS = 1e-06
SOFT_CAP = 50.0
SCORE_SCALE = 1.0 / (12.0 * SOFT_CAP)
MESH = pl.DeviceIdType.MESH
F32 = jnp.float32
BF16 = jnp.bfloat16
NT = (((1,), (1,)), ((), ()))
GELU_C = math.sqrt(2.0 / math.pi)


def rms_scale(values):
    return values * lax.rsqrt(jnp.mean(values * values, axis=-1, keepdims=True) + EPS)


def weights_of(scores):
    return jnp.exp(SOFT_CAP * jnp.tanh(scores * SCORE_SCALE))


def chunks(total, size):
    return [(start, min(size, total - start)) for start in range(0, total, size)]


def kernel(
    n_req, n_mlp,
    tok, attn_gain, post_attn_gain, ffn_gain, post_ffn_gain, wpos, pos, emask, sink_k, sink_v,
    wk_hbm, wv_hbm, wq_hbm, wkey_hbm, wval_hbm, wo_hbm, wg_hbm, wu_hbm, wd_hbm,
    out,
    win_k, win_v, wq, wkey, wval, wo, wg, wu, wd, load_sem,
    ag1, xf, xb, qbuf, ekf, evf, psend, prec,
    pj, s1, r1, s3, r3,
    ag2, hid, acc,
    t1, u1, t2, u2, t3f, t3, u3,
    ss_ag1z, rs_ag1z, ss_ag1c, rs_ag1c, ss_q, rs_q, ss_p, rs_p,
    ss_1, rs_1, ss_3, rs_3,
    ss_ag2z, rs_ag2z, ss_ag2r, rs_ag2r, ss_ag2c, rs_ag2c,
    ss_t1, rs_t1, ss_t2, rs_t2, ss_t3, rs_t3,
):
    n_z = n_mlp // 2
    rq = lax.axis_index("req")
    me = lax.axis_index("mlp")
    z = me // 2
    c = me % 2
    oc = 1 - c
    sib = z * 2 + oc
    tp, width = tok.shape
    group = tp * n_mlp
    total = group * n_req
    kv_cols = wkey.shape[1]
    q_cols = wq.shape[1]
    kv_heads = kv_cols // HD
    ff = wg.shape[0]

    def z_peer(step):
        return {"mlp": lax.rem(z + step, n_z) * 2 + c}

    def r_peer(step):
        return lax.rem(rq + step, n_req)

    loads = {}
    for number, (name, src, dst) in enumerate((
        ("q", wq_hbm, wq), ("k", wkey_hbm, wkey), ("v", wval_hbm, wval),
        ("wk", wk_hbm, win_k), ("wv", wv_hbm, win_v), ("o", wo_hbm, wo),
        ("g", wg_hbm, wg), ("u", wu_hbm, wu), ("d", wd_hbm, wd),
    )):
        loads[name] = pltpu.make_async_copy(src, dst, load_sem.at[number])
        loads[name].start()

    barrier = pltpu.get_barrier_semaphore()
    pl.semaphore_signal(barrier, inc=1, device_id={"mlp": sib}, device_id_type=MESH)
    for step in range(1, n_z):
        pl.semaphore_signal(barrier, inc=1, device_id=z_peer(step), device_id_type=MESH)
    for step in range(1, n_req):
        pl.semaphore_signal(barrier, inc=1, device_id={"req": r_peer(step)}, device_id_type=MESH)

    sent = []

    def send(src, dst, send_sem, recv_sem, device):
        copy = pltpu.make_async_remote_copy(
            src_ref=src, dst_ref=dst, send_sem=send_sem, recv_sem=recv_sem,
            device_id=device, device_id_type=MESH,
        )
        copy.start()
        sent.append(copy)
        return copy

    token_float = tok[...].astype(F32)
    ag1[c, z] = (rms_scale(token_float) * attn_gain[...]).astype(BF16)
    pl.semaphore_wait(barrier, n_z + n_req - 1)
    z_copies = [
        send(ag1.at[c, z], ag1.at[c, z], ss_ag1z.at[k], rs_ag1z.at[k], z_peer(k))
        for k in range(1, n_z)
    ]
    c_copies = [send(ag1.at[c, z], ag1.at[c, z], ss_ag1c.at[0], rs_ag1c.at[0], {"mlp": sib})]
    for k, copy in enumerate(z_copies, 1):
        copy.wait_recv()
        block = ag1.at[c, lax.rem(z + n_z - k, n_z)]
        c_copies.append(send(block, block, ss_ag1c.at[k], rs_ag1c.at[k], {"mlp": sib}))
    for copy in c_copies:
        copy.wait_recv()
    for core in range(2):
        for level in range(n_z):
            row = (level * 2 + core) * tp
            xf[row:row + tp, :] = ag1[core, level].astype(F32)
    rows = xf[0:group, :].astype(BF16)

    loads["q"].wait()
    qbuf[rq] = jnp.dot(rows, wq[...], preferred_element_type=F32).astype(BF16)
    q_copies = [
        send(qbuf.at[rq], qbuf.at[rq], ss_q.at[k], rs_q.at[k], {"req": r_peer(k)})
        for k in range(1, n_req)
    ]
    loads["k"].wait()
    key_new = jnp.dot(rows, wkey[...], preferred_element_type=F32).astype(BF16)
    loads["v"].wait()
    value_new = jnp.dot(rows, wval[...], preferred_element_type=F32).astype(BF16)
    n_sink = sink_k.shape[0]
    for target, new, sinks in ((ekf, key_new, sink_k), (evf, value_new, sink_v)):
        target[...] = jnp.zeros_like(target)
        target[0:group, :] = new.astype(F32)
        target[group:group + n_sink, :] = sinks[...].astype(F32)

    own_q = qbuf[rq]
    extra_k = ekf[...].astype(BF16)
    extra_v = evf[...].astype(BF16)
    own_num, own_den = [], []
    for j in range(kv_heads):
        lanes = slice(j * HD, (j + 1) * HD)
        pair = jnp.concatenate(
            [own_q[:, (2 * j + i) * HD:(2 * j + i + 1) * HD] for i in range(2)], axis=0)
        scores = lax.dot_general(pair, extra_k[:, lanes], NT, preferred_element_type=F32)
        weight = jnp.where(emask[...] > 0, weights_of(scores), 0.0)
        den = jnp.sum(weight, axis=-1, keepdims=True)
        num = jnp.dot(weight.astype(BF16), extra_v[:, lanes], preferred_element_type=F32)
        for i in range(2):
            own_num.append(num[i * group:(i + 1) * group])
            own_den.append(den[i * group:(i + 1) * group])

    loads["wk"].wait()
    loads["wv"].wait()
    for copy in q_copies:
        copy.wait_recv()
    all_q = qbuf[...].reshape(total, q_cols)
    visible = wpos[...] > pos[...]
    lane = lax.broadcasted_iota(jnp.int32, (total, HD), 1)
    den_all = jnp.zeros((total, HD), F32)
    for j in range(kv_heads):
        lanes = slice(j * HD, (j + 1) * HD)
        pair = jnp.concatenate(
            [all_q[:, (2 * j + i) * HD:(2 * j + i + 1) * HD] for i in range(2)], axis=0)
        scores = lax.dot_general(pair, win_k[:, lanes], NT, preferred_element_type=F32)
        weight = jnp.where(visible, weights_of(scores), 0.0)
        den = jnp.sum(weight, axis=-1, keepdims=True)
        num = jnp.dot(weight.astype(BF16), win_v[:, lanes], preferred_element_type=F32)
        for i in range(2):
            h = 2 * j + i
            psend[:, :, h * HD:(h + 1) * HD] = num[i * total:(i + 1) * total].reshape(n_req, group, HD)
            den_all = jnp.where(lane == h, den[i * total:(i + 1) * total], den_all)
    psend[:, :, q_cols:q_cols + HD] = den_all.reshape(n_req, group, HD)
    p_copies = [
        send(psend.at[r_peer(k)], prec.at[k - 1], ss_p.at[k], rs_p.at[k], {"req": r_peer(k)})
        for k in range(1, n_req)
    ]
    partial = psend[rq]
    for k, copy in enumerate(p_copies, 1):
        copy.wait_recv()
        partial = partial + prec[k - 1]
    heads = []
    for h in range(2 * kv_heads):
        num = own_num[h] + partial[:, h * HD:(h + 1) * HD]
        den = own_den[h] + partial[:, q_cols + h:q_cols + h + 1]
        heads.append((num / den).astype(BF16))
    attended = jnp.concatenate(heads, axis=1)
    loads["o"].wait()
    for start, size in chunks(width, 512):
        pj[:, start:start + size] = jnp.dot(
            attended, wo[:, start:start + size], preferred_element_type=F32)

    for core in range(2):
        for level in range(n_z):
            row = (level * 2 + core) * tp
            s1[core, level] = pj[row:row + tp, :].astype(BF16)
    send(s1.at[oc], r1, ss_1, rs_1, {"mlp": sib}).wait_recv()
    for level in range(n_z):
        s3[level] = (s1[c, level].astype(F32) + r1[level].astype(F32)).astype(BF16)
    copies = [
        send(s3.at[lax.rem(z + k, n_z)], r3.at[k - 1], ss_3.at[k], rs_3.at[k], z_peer(k))
        for k in range(1, n_z)
    ]
    head_total = s1[c, z].astype(F32) + r1[z].astype(F32)
    for k, copy in enumerate(copies, 1):
        copy.wait_recv()
        head_total = head_total + r3[k - 1].astype(F32)
    residual = token_float + rms_scale(head_total) * post_attn_gain[...]

    mine = c * n_req + rq
    ag2[mine, z] = (rms_scale(residual) * ffn_gain[...]).astype(BF16)
    copies = [
        send(ag2.at[mine, z], ag2.at[mine, z], ss_ag2z.at[k], rs_ag2z.at[k], z_peer(k))
        for k in range(1, n_z)
    ]
    for copy in copies:
        copy.wait_recv()
    r_copies = [
        send(ag2.at[mine], ag2.at[mine], ss_ag2r.at[k], rs_ag2r.at[k], {"req": r_peer(k)})
        for k in range(1, n_req)
    ]
    c_copies = [send(ag2.at[mine], ag2.at[mine], ss_ag2c.at[0], rs_ag2c.at[0], {"mlp": sib})]
    for k, copy in enumerate(r_copies, 1):
        copy.wait_recv()
        block = ag2.at[c * n_req + lax.rem(rq + n_req - k, n_req)]
        c_copies.append(send(block, block, ss_ag2c.at[k], rs_ag2c.at[k], {"mlp": sib}))
    for copy in c_copies:
        copy.wait_recv()
    for core in range(2):
        for r in range(n_req):
            for level in range(n_z):
                row = r * group + (level * 2 + core) * tp
                xf[row:row + tp, :] = ag2[core * n_req + r, level].astype(F32)
    xb[...] = xf[...].astype(BF16)

    loads["g"].wait()
    loads["u"].wait()

    def ffn_hidden(start, size):
        gate = lax.dot_general(
            xb[...], wg[pl.ds(start, size), :], NT, preferred_element_type=F32)
        up = lax.dot_general(
            xb[...], wu[pl.ds(start, size), :], NT, preferred_element_type=F32)
        inner = GELU_C * (gate + 0.044715 * (gate * gate * gate))
        hid[:, pl.ds(start, size)] = (0.5 * gate * (1.0 + jnp.tanh(inner)) * up).astype(BF16)

    if ff >= 256:
        @pl.loop(0, ff // 256)
        def _(step):
            ffn_hidden(pl.multiple_of(step * 256, 256), 256)
    if ff % 256:
        ffn_hidden(ff - ff % 256, ff % 256)
    loads["d"].wait()

    @pl.loop(0, width // 512)
    def _(step):
        lanes = pl.ds(pl.multiple_of(step * 512, 512), 512)
        acc[:, lanes] = jnp.dot(hid[...], wd[:, lanes], preferred_element_type=F32)

    for core in range(2):
        for r in range(n_req):
            for level in range(n_z):
                row = r * group + (level * 2 + core) * tp
                t1[core, r, level] = acc[row:row + tp, :].astype(BF16)
    order = [r_peer(k) for k in list(range(1, n_req)) + [0]]
    first = [
        send(t1.at[oc, r], u1.at[r], ss_t1.at[k], rs_t1.at[k], {"mlp": sib})
        for k, r in enumerate(order)
    ]
    second = []
    for k, r in enumerate(order):
        first[k].wait_recv()
        both = t1[c, r].astype(F32) + u1[r].astype(F32)
        if k < n_req - 1:
            t2[r] = both.astype(BF16)
            second.append(send(
                t2.at[r], u2.at[k], ss_t2.at[k], rs_t2.at[k], {"req": r}))
    for k, copy in enumerate(second):
        copy.wait_recv()
        both = both + u2[k].astype(F32)
    t3f[...] = both
    t3[...] = both.astype(BF16)
    copies = [
        send(t3.at[lax.rem(z + k, n_z)], u3.at[k - 1], ss_t3.at[k], rs_t3.at[k], z_peer(k))
        for k in range(1, n_z)
    ]
    ffn_out = t3f[z]
    for k, copy in enumerate(copies, 1):
        copy.wait_recv()
        ffn_out = ffn_out + u3[k - 1].astype(F32)
    out[...] = (residual + rms_scale(ffn_out) * post_ffn_gain[...]).astype(BF16)
    for copy in sent:
        copy.wait_send()


def positions(seg_rows):
    ordering = jnp.arange(seg_rows.shape[-1], dtype=jnp.int32)
    same_seg = seg_rows[..., :, None] == seg_rows[..., None, :]
    earlier = ordering[None, :] < ordering[:, None]
    return jnp.sum((same_seg & earlier).astype(jnp.int32), axis=-1)


def shards(
    n_req, n_mlp,
    tokens, segments, owners, sink_keys, sink_values, window_keys, window_values,
    attn_gain, post_attn_gain, ffn_gain, post_ffn_gain,
    w_query, w_key, w_value, w_out, w_gate, w_up, w_down,
):
    tp, width = tokens.shape
    n_z = n_mlp // 2
    group = tp * n_mlp
    total = group * n_req
    block = window_keys.shape[0]
    q_cols, kv_cols, ff = w_query.shape[1], w_key.shape[1], w_gate.shape[0]
    n_sink = sink_keys.shape[0]
    extra = 2 * group
    req = lax.axis_index("req")
    pos = positions(segments).reshape(total, 1)
    pos = jnp.concatenate([pos, pos], axis=0)
    owner = jnp.sum(jnp.where(jnp.arange(n_req) == req, owners, 0))
    wpos = (owner * block + jnp.arange(block, dtype=jnp.int32)).reshape(1, block)
    seg = lax.dynamic_index_in_dim(segments, req, 0, keepdims=False)
    order = jnp.arange(group, dtype=jnp.int32)
    local = (seg[:, None] == seg[None, :]) & (order[None, :] <= order[:, None])
    sinks = jnp.broadcast_to(jnp.arange(extra - group) < n_sink, (group, extra - group))
    emask = jnp.concatenate([local, sinks], axis=1).astype(jnp.int32)
    emask = jnp.concatenate([emask, emask], axis=0)

    def v(shape, dtype=BF16):
        return pltpu.VMEM(shape, dtype)

    dma = pltpu.SemaphoreType.DMA
    scratch = [v(a.shape) for a in (
        window_keys, window_values, w_query, w_key, w_value, w_out, w_gate, w_up, w_down)]
    scratch += [
        dma((9,)),
        v((2, n_z, tp, width)), v((total, width), F32), v((total, width)),
        v((n_req, group, q_cols)), v((extra, kv_cols), F32), v((extra, kv_cols), F32),
        v((n_req, group, q_cols + HD), F32), v((max(n_req - 1, 1), group, q_cols + HD), F32),
        v((group, width), F32), v((2, n_z, tp, width)), v((n_z, tp, width)),
        v((n_z, tp, width)), v((n_z - 1, tp, width)),
        v((2 * n_req, n_z, tp, width)), v((total, ff)), v((total, width), F32),
        v((2, n_req, n_z, tp, width)), v((n_req, n_z, tp, width)),
        v((n_req, n_z, tp, width)), v((n_req - 1, n_z, tp, width)),
        v((n_z, tp, width), F32), v((n_z, tp, width)), v((n_z - 1, tp, width)),
        dma((n_z,)), dma((n_z,)), dma((n_z,)), dma((n_z,)),
        dma((n_req,)), dma((n_req,)), dma((n_req,)), dma((n_req,)),
        dma, dma, dma((n_z,)), dma((n_z,)),
        dma((n_z,)), dma((n_z,)), dma((n_req,)), dma((n_req,)), dma((n_req,)), dma((n_req,)),
        dma((n_req,)), dma((n_req,)), dma((n_req,)), dma((n_req,)), dma((n_z,)), dma((n_z,)),
    ]
    vmem = pl.BlockSpec(memory_space=pltpu.VMEM)
    hbm = pl.BlockSpec(memory_space=pl.ANY)
    return pl.pallas_call(
        functools.partial(kernel, n_req, n_mlp),
        name="layer",
        out_shape=jax.ShapeDtypeStruct((tp, width), BF16),
        in_specs=[vmem] * 10 + [hbm] * 9,
        out_specs=vmem,
        scratch_shapes=scratch,
        compiler_params=pltpu.CompilerParams(
            collective_id=0, has_side_effects=True, vmem_limit_bytes=62 << 20),
    )(
        tokens, attn_gain[None], post_attn_gain[None], ffn_gain[None], post_ffn_gain[None],
        wpos, pos, emask, sink_keys, sink_values,
        window_keys, window_values, w_query, w_key, w_value, w_out, w_gate, w_up, w_down,
    )


def solution(mesh):
    both = P(("req", "mlp"), None)
    return jax.shard_map(
        functools.partial(shards, mesh.shape["req"], mesh.shape["mlp"]),
        mesh=mesh,
        in_specs=(
            both, P(), P(), P(None, "mlp"), P(None, "mlp"), P("req", "mlp"), P("req", "mlp"),
            P(), P(), P(), P(),
            P(None, "mlp"), P(None, "mlp"), P(None, "mlp"), P("mlp", None), both, both, both,
        ),
        out_specs=both,
        check_vma=False,
    )
```

```python
import functools
import math

import jax
import jax.numpy as jnp
from jax import lax
from jax.experimental import pallas as pl
from jax.experimental.pallas import tpu as pltpu
from jax.sharding import PartitionSpec as P

HD = 128
EPS = 1e-06
SOFT_CAP = 50.0
SCORE_SCALE = 1.0 / (12.0 * SOFT_CAP)
MESH = pl.DeviceIdType.MESH
F32 = jnp.float32
BF16 = jnp.bfloat16
NT = (((1,), (1,)), ((), ()))
GELU_C = math.sqrt(2.0 / math.pi)


def rms_scale(values):
    return values * lax.rsqrt(jnp.mean(values * values, axis=-1, keepdims=True) + EPS)


def weights_of(scores):
    return jnp.exp(SOFT_CAP * jnp.tanh(scores * SCORE_SCALE))


def chunks(total, size):
    return [(start, min(size, total - start)) for start in range(0, total, size)]


def kernel(
    n_req, n_mlp,
    tok, segments, owners, sink_k, sink_v, gains_a, gains_pa, gains_f, gains_pf,
    wk_hbm, wv_hbm, wq_hbm, wkey_hbm, wval_hbm, wo_hbm, wg_hbm, wu_hbm, wd_hbm,
    out,
    win_k, win_v, wq, wkey, wval, wo, wg, wu, wd,
    attn_gain, post_attn_gain, ffn_gain, post_ffn_gain, load_sem,
    posv, segv,
    ag1, xf, xb, qbuf, ekf, evf, psend, prec,
    pj, s1, r1, s3, r3,
    ag2, hid, acc,
    t1, u1, t2, u2, t3f, t3, u3,
    ss_ag1z, rs_ag1z, ss_ag1c, rs_ag1c, ss_q, rs_q, ss_p, rs_p,
    ss_1, rs_1, ss_3, rs_3,
    ss_ag2z, rs_ag2z, ss_ag2r, rs_ag2r, ss_ag2c, rs_ag2c,
    ss_t1, rs_t1, ss_t2, rs_t2, ss_t3, rs_t3,
):
    n_z = n_mlp // 2
    rq = lax.axis_index("req")
    me = lax.axis_index("mlp")
    z = me // 2
    c = me % 2
    oc = 1 - c
    sib = z * 2 + oc
    tp, width = tok.shape
    group = tp * n_mlp
    total = group * n_req
    kv_cols = wkey.shape[1]
    q_cols = wq.shape[1]
    kv_heads = kv_cols // HD
    ff = wg.shape[0]

    def z_peer(step):
        return {"mlp": lax.rem(z + step, n_z) * 2 + c}

    def r_peer(step):
        return lax.rem(rq + step, n_req)

    loads = {}
    for number, (name, src, dst) in enumerate((
        ("ga", gains_a, attn_gain.at[0]), ("gpa", gains_pa, post_attn_gain.at[0]),
        ("gf", gains_f, ffn_gain.at[0]), ("gpf", gains_pf, post_ffn_gain.at[0]),
        ("q", wq_hbm, wq), ("k", wkey_hbm, wkey), ("v", wval_hbm, wval),
        ("wk", wk_hbm, win_k), ("wv", wv_hbm, win_v), ("o", wo_hbm, wo),
        ("g", wg_hbm, wg), ("u", wu_hbm, wu), ("d", wd_hbm, wd),
    )):
        loads[name] = pltpu.make_async_copy(src, dst, load_sem.at[number])
        if name not in ("g", "u", "d"):
            loads[name].start()

    barrier = pltpu.get_barrier_semaphore()
    pl.semaphore_signal(barrier, inc=1, device_id={"mlp": sib}, device_id_type=MESH)
    for step in range(1, n_z):
        pl.semaphore_signal(barrier, inc=1, device_id=z_peer(step), device_id_type=MESH)
    for step in range(1, n_req):
        pl.semaphore_signal(barrier, inc=1, device_id={"req": r_peer(step)}, device_id_type=MESH)

    sent = []

    def send(src, dst, send_sem, recv_sem, device):
        copy = pltpu.make_async_remote_copy(
            src_ref=src, dst_ref=dst, send_sem=send_sem, recv_sem=recv_sem,
            device_id=device, device_id_type=MESH,
        )
        copy.start()
        sent.append(copy)
        return copy

    token_float = tok[...].astype(F32)
    loads["ga"].wait()
    ag1[c, z] = (rms_scale(token_float) * attn_gain[...]).astype(BF16)
    pl.semaphore_wait(barrier, n_z + n_req - 1)
    z_copies = [
        send(ag1.at[c, z], ag1.at[c, z], ss_ag1z.at[k], rs_ag1z.at[k], z_peer(k))
        for k in range(1, n_z)
    ]
    c_copies = [send(ag1.at[c, z], ag1.at[c, z], ss_ag1c.at[0], rs_ag1c.at[0], {"mlp": sib})]
    for g in range(n_req):
        at = jnp.int32(0)
        for t in range(group):
            if t:
                at = jnp.where(segments[g, t] == segments[g, t - 1], at + 1, 0)
            posv[g * group + t:g * group + t + 1, :] = jnp.full((1, HD), at, jnp.int32)
    extra = 2 * group
    column = lax.broadcasted_iota(jnp.int32, (group, extra), 1)
    row_of = lax.broadcasted_iota(jnp.int32, (group, extra), 0)
    seg_row = jnp.full((group, extra), -1, jnp.int32)
    for t in range(group):
        segv[t:t + 1, :] = jnp.full((1, extra), segments[rq, t], jnp.int32)
        seg_row = jnp.where(column == t, segments[rq, t], seg_row)
    n_sink = sink_k.shape[0]
    local = (segv[...] == seg_row) & (column <= row_of)
    sinks = (column >= group) & (column < group + n_sink)
    one = jnp.where(local | sinks, 1, 0)
    emask = jnp.concatenate([one, one], axis=0) > 0
    block_rows = win_k.shape[0]
    wpos = owners[rq] * block_rows + lax.broadcasted_iota(jnp.int32, (1, block_rows), 1)
    for k, copy in enumerate(z_copies, 1):
        copy.wait_recv()
        block = ag1.at[c, lax.rem(z + n_z - k, n_z)]
        c_copies.append(send(block, block, ss_ag1c.at[k], rs_ag1c.at[k], {"mlp": sib}))
    for copy in c_copies:
        copy.wait_recv()
    for core in range(2):
        for level in range(n_z):
            row = (level * 2 + core) * tp
            xf[row:row + tp, :] = ag1[core, level].astype(F32)
    rows = xf[0:group, :].astype(BF16)

    loads["q"].wait()
    qbuf[rq] = jnp.dot(rows, wq[...], preferred_element_type=F32).astype(BF16)
    q_copies = [
        send(qbuf.at[rq], qbuf.at[rq], ss_q.at[k], rs_q.at[k], {"req": r_peer(k)})
        for k in range(1, n_req)
    ]
    loads["k"].wait()
    key_new = jnp.dot(rows, wkey[...], preferred_element_type=F32).astype(BF16)
    loads["v"].wait()
    for name in ("g", "u", "d"):
        loads[name].start()
    value_new = jnp.dot(rows, wval[...], preferred_element_type=F32).astype(BF16)
    for target, new, sinks in ((ekf, key_new, sink_k), (evf, value_new, sink_v)):
        target[...] = jnp.zeros_like(target)
        target[0:group, :] = new.astype(F32)
        target[group:group + n_sink, :] = sinks[...].astype(F32)

    own_q = qbuf[rq]
    extra_k = ekf[...].astype(BF16)
    extra_v = evf[...].astype(BF16)
    own_num, own_den = [], []
    for j in range(kv_heads):
        lanes = slice(j * HD, (j + 1) * HD)
        pair = jnp.concatenate(
            [own_q[:, (2 * j + i) * HD:(2 * j + i + 1) * HD] for i in range(2)], axis=0)
        scores = lax.dot_general(pair, extra_k[:, lanes], NT, preferred_element_type=F32)
        weight = jnp.where(emask, weights_of(scores), 0.0)
        den = jnp.sum(weight, axis=-1, keepdims=True)
        num = jnp.dot(weight.astype(BF16), extra_v[:, lanes], preferred_element_type=F32)
        for i in range(2):
            own_num.append(num[i * group:(i + 1) * group])
            own_den.append(den[i * group:(i + 1) * group])

    loads["wk"].wait()
    loads["wv"].wait()
    for copy in q_copies:
        copy.wait_recv()
    all_q = qbuf[...].reshape(total, q_cols)
    visible = wpos > posv[:, 0:1]
    visible = jnp.where(visible, 1, 0)
    visible = jnp.concatenate([visible, visible], axis=0) > 0
    lane = lax.broadcasted_iota(jnp.int32, (total, HD), 1)
    den_all = jnp.zeros((total, HD), F32)
    for j in range(kv_heads):
        lanes = slice(j * HD, (j + 1) * HD)
        pair = jnp.concatenate(
            [all_q[:, (2 * j + i) * HD:(2 * j + i + 1) * HD] for i in range(2)], axis=0)
        scores = lax.dot_general(pair, win_k[:, lanes], NT, preferred_element_type=F32)
        weight = jnp.where(visible, weights_of(scores), 0.0)
        den = jnp.sum(weight, axis=-1, keepdims=True)
        num = jnp.dot(weight.astype(BF16), win_v[:, lanes], preferred_element_type=F32)
        for i in range(2):
            h = 2 * j + i
            psend[:, :, h * HD:(h + 1) * HD] = num[i * total:(i + 1) * total].reshape(n_req, group, HD)
            den_all = jnp.where(lane == h, den[i * total:(i + 1) * total], den_all)
    psend[:, :, q_cols:q_cols + HD] = den_all.reshape(n_req, group, HD)
    p_copies = [
        send(psend.at[r_peer(k)], prec.at[k - 1], ss_p.at[k], rs_p.at[k], {"req": r_peer(k)})
        for k in range(1, n_req)
    ]
    partial = psend[rq]
    for k, copy in enumerate(p_copies, 1):
        copy.wait_recv()
        partial = partial + prec[k - 1]
    heads = []
    for h in range(2 * kv_heads):
        num = own_num[h] + partial[:, h * HD:(h + 1) * HD]
        den = own_den[h] + partial[:, q_cols + h:q_cols + h + 1]
        heads.append((num / den).astype(BF16))
    attended = jnp.concatenate(heads, axis=1)
    loads["o"].wait()
    for start, size in chunks(width, 512):
        pj[:, start:start + size] = jnp.dot(
            attended, wo[:, start:start + size], preferred_element_type=F32)

    for core in range(2):
        for level in range(n_z):
            row = (level * 2 + core) * tp
            s1[core, level] = pj[row:row + tp, :].astype(BF16)
    send(s1.at[oc], r1, ss_1, rs_1, {"mlp": sib}).wait_recv()
    for level in range(n_z):
        s3[level] = (s1[c, level].astype(F32) + r1[level].astype(F32)).astype(BF16)
    copies = [
        send(s3.at[lax.rem(z + k, n_z)], r3.at[k - 1], ss_3.at[k], rs_3.at[k], z_peer(k))
        for k in range(1, n_z)
    ]
    head_total = s1[c, z].astype(F32) + r1[z].astype(F32)
    for k, copy in enumerate(copies, 1):
        copy.wait_recv()
        head_total = head_total + r3[k - 1].astype(F32)
    for name in ("gpa", "gf", "gpf"):
        loads[name].wait()
    residual = token_float + rms_scale(head_total) * post_attn_gain[...]

    ag2[0, 0, z] = (rms_scale(residual) * ffn_gain[...]).astype(BF16)
    z_copies = [
        send(ag2.at[0, 0, z], ag2.at[0, 0, z], ss_ag2z.at[k], rs_ag2z.at[k], z_peer(k))
        for k in range(1, n_z)
    ]
    r_copies = {}
    for step in range(n_z):
        if step:
            z_copies[step - 1].wait_recv()
        level = lax.rem(z + n_z - step, n_z)
        for k in range(1, n_req):
            r_copies[step, k] = send(
                ag2.at[0, 0, level], ag2.at[0, k, level], ss_ag2r.at[step, k],
                rs_ag2r.at[step, k], {"req": r_peer(k)})
    c_copies = [send(ag2.at[0, 0], ag2.at[1, 0], ss_ag2c.at[0], rs_ag2c.at[0], {"mlp": sib})]
    span = n_z * tp

    def unpack(core, k):
        base = (core * n_req + k) * span
        for level in range(n_z):
            xf[base + level * tp:base + (level + 1) * tp, :] = ag2[core, k, level].astype(F32)

    unpack(0, 0)
    for k in range(1, n_req):
        for step in range(n_z):
            r_copies[step, k].wait_recv()
        c_copies.append(send(
            ag2.at[0, k], ag2.at[1, k], ss_ag2c.at[k], rs_ag2c.at[k], {"mlp": sib}))
        unpack(0, k)
    for k, copy in enumerate(c_copies):
        copy.wait_recv()
        unpack(1, k)
    xb[...] = xf[...].astype(BF16)

    loads["g"].wait()
    loads["u"].wait()

    def ffn_hidden(start, size):
        gate = lax.dot_general(
            xb[...], wg[pl.ds(start, size), :], NT, preferred_element_type=F32)
        up = lax.dot_general(
            xb[...], wu[pl.ds(start, size), :], NT, preferred_element_type=F32)
        inner = GELU_C * (gate + 0.044715 * (gate * gate * gate))
        hid[:, pl.ds(start, size)] = (0.5 * gate * (1.0 + jnp.tanh(inner)) * up).astype(BF16)

    if ff >= 256:
        @pl.loop(0, ff // 256)
        def _(step):
            ffn_hidden(pl.multiple_of(step * 256, 256), 256)
    if ff % 256:
        ffn_hidden(ff - ff % 256, ff % 256)
    loads["d"].wait()

    parts, cols = t1.shape[1], t1.shape[-1]
    order = list(range(1, n_req)) + [0]
    first, second, third, kept, finals = {}, {}, {}, {}, {}

    def partial_sums(j):
        @pl.loop(0, cols // 512)
        def _(step):
            start = pl.multiple_of(step * 512, 512)
            acc[j, :, pl.ds(start, 512)] = jnp.dot(
                hid[...], wd[:, pl.ds(j * cols + start, 512)], preferred_element_type=F32)

        for core in (1, 0):
            for k in order:
                base = (core * n_req + k) * span
                for level in range(n_z):
                    row = base + level * tp
                    t1[core, j, k, level] = acc[j, row:row + tp, :].astype(BF16)
                if core:
                    first[j, k] = send(
                        t1.at[1, j, k], u1.at[j, k], ss_t1.at[j, k], rs_t1.at[j, k], {"mlp": sib})

    def add_cores(j):
        for k in order:
            first[j, k].wait_recv()
            both = t1[0, j, k].astype(F32) + u1[j, k].astype(F32)
            if k:
                t2[j, k] = both.astype(BF16)
                second[j, k] = send(
                    t2.at[j, k], u2.at[j, k], ss_t2.at[j, k], rs_t2.at[j, k],
                    {"req": r_peer(n_req - k)})
            else:
                t3f[j] = both

    def add_req(j):
        both = t3f[j]
        for k in range(1, n_req):
            second[j, k].wait_recv()
            both = both + u2[j, k].astype(F32)
        t3f[j] = both
        t3[j] = both.astype(BF16)
        for k in range(1, n_z):
            third[j, k] = send(
                t3.at[j, lax.rem(z + k, n_z)], u3.at[j, k], ss_t3.at[j, k], rs_t3.at[j, k],
                z_peer(k))

    for j in range(parts + 2):
        if j < parts:
            partial_sums(j)
        if 0 <= j - 1 < parts:
            add_cores(j - 1)
        if 0 <= j - 2 < parts:
            add_req(j - 2)
    squares = jnp.zeros((tp, 1), F32)
    for j in range(parts):
        total_j = t3f[j, z]
        for k in range(1, n_z):
            third[j, k].wait_recv()
            total_j = total_j + u3[j, k].astype(F32)
        finals[j] = total_j
        squares = squares + jnp.sum(total_j * total_j, axis=-1, keepdims=True)
    scale = lax.rsqrt(squares / width + EPS)
    for j in range(parts):
        lanes = slice(j * cols, (j + 1) * cols)
        out[:, lanes] = (
            residual[:, lanes] + finals[j] * scale * post_ffn_gain[:, lanes]).astype(BF16)
    for copy in sent:
        copy.wait_send()


def shards(
    n_req, n_mlp,
    tokens, segments, owners, sink_keys, sink_values, window_keys, window_values,
    attn_gain, post_attn_gain, ffn_gain, post_ffn_gain,
    w_query, w_key, w_value, w_out, w_gate, w_up, w_down,
):
    tp, width = tokens.shape
    n_z = n_mlp // 2
    group = tp * n_mlp
    total = group * n_req
    q_cols, kv_cols, ff = w_query.shape[1], w_key.shape[1], w_gate.shape[0]
    extra = 2 * group
    parts = 3
    cols = width // parts
    def v(shape, dtype=BF16):
        return pltpu.VMEM(shape, dtype)

    dma = pltpu.SemaphoreType.DMA
    scratch = [v(a.shape) for a in (
        window_keys, window_values, w_query, w_key, w_value, w_out, w_gate, w_up, w_down)]
    scratch += [v((1, width), F32)] * 4
    scratch += [
        dma((13,)),
        v((total, HD), jnp.int32), v((group, extra), jnp.int32),
        v((2, n_z, tp, width)), v((total, width), F32), v((total, width)),
        v((n_req, group, q_cols)), v((extra, kv_cols), F32), v((extra, kv_cols), F32),
        v((n_req, group, q_cols + HD), F32), v((max(n_req - 1, 1), group, q_cols + HD), F32),
        v((group, width), F32), v((2, n_z, tp, width)), v((n_z, tp, width)),
        v((n_z, tp, width)), v((n_z - 1, tp, width)),
        v((2, n_req, n_z, tp, width)), v((total, ff)), v((parts, total, cols), F32),
        v((2, parts, n_req, n_z, tp, cols)), v((parts, n_req, n_z, tp, cols)),
        v((parts, n_req, n_z, tp, cols)), v((parts, n_req, n_z, tp, cols)),
        v((parts, n_z, tp, cols), F32), v((parts, n_z, tp, cols)), v((parts, n_z, tp, cols)),
        dma((n_z,)), dma((n_z,)), dma((n_z,)), dma((n_z,)),
        dma((n_req,)), dma((n_req,)), dma((n_req,)), dma((n_req,)),
        dma, dma, dma((n_z,)), dma((n_z,)),
        dma((n_z,)), dma((n_z,)), dma((n_z, n_req)), dma((n_z, n_req)),
        dma((n_req,)), dma((n_req,)),
        dma((parts, n_req)), dma((parts, n_req)), dma((parts, n_req)), dma((parts, n_req)),
        dma((parts, n_z)), dma((parts, n_z)),
    ]
    vmem = pl.BlockSpec(memory_space=pltpu.VMEM)
    smem = pl.BlockSpec(memory_space=pltpu.SMEM)
    hbm = pl.BlockSpec(memory_space=pl.ANY)
    return pl.pallas_call(
        functools.partial(kernel, n_req, n_mlp),
        name="layer",
        out_shape=jax.ShapeDtypeStruct((tp, width), BF16),
        in_specs=[vmem, smem, smem, vmem, vmem] + [hbm] * 13,
        out_specs=vmem,
        scratch_shapes=scratch,
        compiler_params=pltpu.CompilerParams(
            collective_id=0, has_side_effects=True, vmem_limit_bytes=62 << 20),
    )(
        tokens, segments, owners, sink_keys, sink_values,
        attn_gain, post_attn_gain, ffn_gain, post_ffn_gain,
        window_keys, window_values, w_query, w_key, w_value, w_out, w_gate, w_up, w_down,
    )


def solution(mesh):
    both = P(("req", "mlp"), None)
    return jax.shard_map(
        functools.partial(shards, mesh.shape["req"], mesh.shape["mlp"]),
        mesh=mesh,
        in_specs=(
            both, P(), P(), P(None, "mlp"), P(None, "mlp"), P("req", "mlp"), P("req", "mlp"),
            P(), P(), P(), P(),
            P(None, "mlp"), P(None, "mlp"), P(None, "mlp"), P("mlp", None), both, both, both,
        ),
        out_specs=both,
        check_vma=False,
    )
```

```python
import functools
import math

import jax
import jax.numpy as jnp
from jax import lax
from jax.experimental import pallas as pl
from jax.experimental.pallas import tpu as pltpu
from jax.sharding import PartitionSpec as P

HD = 128
EPS = 1e-06
SOFT_CAP = 50.0
SCORE_SCALE = 1.0 / (12.0 * SOFT_CAP)
MESH = pl.DeviceIdType.MESH
F32 = jnp.float32
BF16 = jnp.bfloat16
NT = (((1,), (1,)), ((), ()))
GELU_C = math.sqrt(2.0 / math.pi)


def rms_scale(values):
    return values * lax.rsqrt(jnp.mean(values * values, axis=-1, keepdims=True) + EPS)


def weights_of(scores):
    return jnp.exp(SOFT_CAP * jnp.tanh(scores * SCORE_SCALE))


def chunks(total, size):
    return [(start, min(size, total - start)) for start in range(0, total, size)]


def kernel(
    n_req, n_mlp,
    tok, segments, owners, sink_k, sink_v, gains_a, gains_pa, gains_f, gains_pf,
    wk_hbm, wv_hbm, wq_hbm, wkey_hbm, wval_hbm, wo_hbm, wg_hbm, wu_hbm, wd_hbm,
    out,
    win_k, win_v, wq, wkey, wval, wo, wg, wu, wd,
    attn_gain, post_attn_gain, ffn_gain, post_ffn_gain, load_sem,
    posv, segv,
    ag1, xf, xb, qbuf, ekf, evf, psend, prec,
    pj, s1, r1, s3, r3,
    ag2, hid, acc,
    t1, u1, t2, u2, t3f, t3, u3,
    ss_ag1z, rs_ag1z, ss_ag1c, rs_ag1c, ss_q, rs_q, ss_p, rs_p,
    ss_1, rs_1, ss_3, rs_3,
    ss_ag2z, rs_ag2z, ss_ag2r, rs_ag2r, ss_ag2c, rs_ag2c,
    ss_t1, rs_t1, ss_t2, rs_t2, ss_t3, rs_t3,
):
    n_z = n_mlp // 2
    rq = lax.axis_index("req")
    me = lax.axis_index("mlp")
    z = me // 2
    c = me % 2
    oc = 1 - c
    sib = z * 2 + oc
    tp, width = tok.shape
    group = tp * n_mlp
    total = group * n_req
    kv_cols = wkey.shape[1]
    q_cols = wq.shape[1]
    kv_heads = kv_cols // HD
    ff = wg.shape[0]

    def z_peer(step):
        return {"mlp": lax.rem(z + step, n_z) * 2 + c}

    def r_peer(step):
        return lax.rem(rq + step, n_req)

    loads = {}
    for number, (name, src, dst) in enumerate((
        ("ga", gains_a, attn_gain.at[0]), ("gpa", gains_pa, post_attn_gain.at[0]),
        ("gf", gains_f, ffn_gain.at[0]), ("gpf", gains_pf, post_ffn_gain.at[0]),
        ("q", wq_hbm, wq), ("k", wkey_hbm, wkey), ("v", wval_hbm, wval),
        ("wk", wk_hbm, win_k), ("wv", wv_hbm, win_v), ("o", wo_hbm, wo),
        ("g", wg_hbm, wg), ("u", wu_hbm, wu), ("d", wd_hbm, wd),
    )):
        loads[name] = pltpu.make_async_copy(src, dst, load_sem.at[number])
        loads[name].start()

    barrier = pltpu.get_barrier_semaphore()
    pl.semaphore_signal(barrier, inc=1, device_id={"mlp": sib}, device_id_type=MESH)
    for step in range(1, n_z):
        pl.semaphore_signal(barrier, inc=1, device_id=z_peer(step), device_id_type=MESH)
    for step in range(1, n_req):
        pl.semaphore_signal(barrier, inc=1, device_id={"req": r_peer(step)}, device_id_type=MESH)

    sent = []

    def send(src, dst, send_sem, recv_sem, device):
        copy = pltpu.make_async_remote_copy(
            src_ref=src, dst_ref=dst, send_sem=send_sem, recv_sem=recv_sem,
            device_id=device, device_id_type=MESH,
        )
        copy.start()
        sent.append(copy)
        return copy

    token_float = tok[...].astype(F32)
    loads["ga"].wait()
    ag1[c, z] = (rms_scale(token_float) * attn_gain[...]).astype(BF16)
    pl.semaphore_wait(barrier, n_z + n_req - 1)
    z_copies = [
        send(ag1.at[c, z], ag1.at[c, z], ss_ag1z.at[k], rs_ag1z.at[k], z_peer(k))
        for k in range(1, n_z)
    ]
    c_copies = [send(ag1.at[c, z], ag1.at[c, z], ss_ag1c.at[0], rs_ag1c.at[0], {"mlp": sib})]
    for g in range(n_req):
        at = jnp.int32(0)
        for t in range(group):
            if t:
                at = jnp.where(segments[g, t] == segments[g, t - 1], at + 1, 0)
            posv[g * group + t:g * group + t + 1, :] = jnp.full((1, HD), at, jnp.int32)
    extra = 2 * group
    column = lax.broadcasted_iota(jnp.int32, (group, extra), 1)
    row_of = lax.broadcasted_iota(jnp.int32, (group, extra), 0)
    seg_row = jnp.full((group, extra), -1, jnp.int32)
    for t in range(group):
        segv[t:t + 1, :] = jnp.full((1, extra), segments[rq, t], jnp.int32)
        seg_row = jnp.where(column == t, segments[rq, t], seg_row)
    n_sink = sink_k.shape[0]
    local = (segv[...] == seg_row) & (column <= row_of)
    sinks = (column >= group) & (column < group + n_sink)
    one = jnp.where(local | sinks, 1, 0)
    emask = jnp.concatenate([one, one], axis=0) > 0
    block_rows = win_k.shape[0]
    wpos = owners[rq] * block_rows + lax.broadcasted_iota(jnp.int32, (1, block_rows), 1)
    for k, copy in enumerate(z_copies, 1):
        copy.wait_recv()
        block = ag1.at[c, lax.rem(z + n_z - k, n_z)]
        c_copies.append(send(block, block, ss_ag1c.at[k], rs_ag1c.at[k], {"mlp": sib}))
    for copy in c_copies:
        copy.wait_recv()
    for core in range(2):
        for level in range(n_z):
            row = (level * 2 + core) * tp
            xf[row:row + tp, :] = ag1[core, level].astype(F32)
    rows = xf[0:group, :].astype(BF16)

    loads["q"].wait()
    qbuf[rq] = jnp.dot(rows, wq[...], preferred_element_type=F32).astype(BF16)
    q_copies = [
        send(qbuf.at[rq], qbuf.at[rq], ss_q.at[k], rs_q.at[k], {"req": r_peer(k)})
        for k in range(1, n_req)
    ]
    loads["k"].wait()
    key_new = jnp.dot(rows, wkey[...], preferred_element_type=F32).astype(BF16)
    loads["v"].wait()
    value_new = jnp.dot(rows, wval[...], preferred_element_type=F32).astype(BF16)
    for target, new, sinks in ((ekf, key_new, sink_k), (evf, value_new, sink_v)):
        target[...] = jnp.zeros_like(target)
        target[0:group, :] = new.astype(F32)
        target[group:group + n_sink, :] = sinks[...].astype(F32)

    own_q = qbuf[rq]
    extra_k = ekf[...].astype(BF16)
    extra_v = evf[...].astype(BF16)
    own_num, own_den = [], []
    for j in range(kv_heads):
        lanes = slice(j * HD, (j + 1) * HD)
        pair = jnp.concatenate(
            [own_q[:, (2 * j + i) * HD:(2 * j + i + 1) * HD] for i in range(2)], axis=0)
        scores = lax.dot_general(pair, extra_k[:, lanes], NT, preferred_element_type=F32)
        weight = jnp.where(emask, weights_of(scores), 0.0)
        den = jnp.sum(weight, axis=-1, keepdims=True)
        num = jnp.dot(weight.astype(BF16), extra_v[:, lanes], preferred_element_type=F32)
        for i in range(2):
            own_num.append(num[i * group:(i + 1) * group])
            own_den.append(den[i * group:(i + 1) * group])

    loads["wk"].wait()
    loads["wv"].wait()
    for copy in q_copies:
        copy.wait_recv()
    all_q = qbuf[...].reshape(total, q_cols)
    visible = wpos > posv[:, 0:1]
    visible = jnp.where(visible, 1, 0)
    visible = jnp.concatenate([visible, visible], axis=0) > 0
    lane = lax.broadcasted_iota(jnp.int32, (total, HD), 1)
    den_all = jnp.zeros((total, HD), F32)
    for j in range(kv_heads):
        lanes = slice(j * HD, (j + 1) * HD)
        pair = jnp.concatenate(
            [all_q[:, (2 * j + i) * HD:(2 * j + i + 1) * HD] for i in range(2)], axis=0)
        scores = lax.dot_general(pair, win_k[:, lanes], NT, preferred_element_type=F32)
        weight = jnp.where(visible, weights_of(scores), 0.0)
        den = jnp.sum(weight, axis=-1, keepdims=True)
        num = jnp.dot(weight.astype(BF16), win_v[:, lanes], preferred_element_type=F32)
        for i in range(2):
            h = 2 * j + i
            psend[:, :, h * HD:(h + 1) * HD] = num[i * total:(i + 1) * total].reshape(n_req, group, HD)
            den_all = jnp.where(lane == h, den[i * total:(i + 1) * total], den_all)
    psend[:, :, q_cols:q_cols + HD] = den_all.reshape(n_req, group, HD)
    p_copies = [
        send(psend.at[r_peer(k)], prec.at[k - 1], ss_p.at[k], rs_p.at[k], {"req": r_peer(k)})
        for k in range(1, n_req)
    ]
    partial = psend[rq]
    for k, copy in enumerate(p_copies, 1):
        copy.wait_recv()
        partial = partial + prec[k - 1]
    heads = []
    for h in range(2 * kv_heads):
        num = own_num[h] + partial[:, h * HD:(h + 1) * HD]
        den = own_den[h] + partial[:, q_cols + h:q_cols + h + 1]
        heads.append((num / den).astype(BF16))
    attended = jnp.concatenate(heads, axis=1)
    loads["o"].wait()
    for start, size in chunks(width, 512):
        pj[:, start:start + size] = jnp.dot(
            attended, wo[:, start:start + size], preferred_element_type=F32)

    for core in range(2):
        for level in range(n_z):
            row = (level * 2 + core) * tp
            s1[core, level] = pj[row:row + tp, :].astype(BF16)
    send(s1.at[oc], r1, ss_1, rs_1, {"mlp": sib}).wait_recv()
    for level in range(n_z):
        s3[level] = (s1[c, level].astype(F32) + r1[level].astype(F32)).astype(BF16)
    copies = [
        send(s3.at[lax.rem(z + k, n_z)], r3.at[k - 1], ss_3.at[k], rs_3.at[k], z_peer(k))
        for k in range(1, n_z)
    ]
    head_total = s1[c, z].astype(F32) + r1[z].astype(F32)
    for k, copy in enumerate(copies, 1):
        copy.wait_recv()
        head_total = head_total + r3[k - 1].astype(F32)
    for name in ("gpa", "gf", "gpf"):
        loads[name].wait()
    residual = token_float + rms_scale(head_total) * post_attn_gain[...]

    ag2[0, 0, z] = (rms_scale(residual) * ffn_gain[...]).astype(BF16)
    z_copies = [
        send(ag2.at[0, 0, z], ag2.at[0, 0, z], ss_ag2z.at[k], rs_ag2z.at[k], z_peer(k))
        for k in range(1, n_z)
    ]
    r_copies = {}
    for step in range(n_z):
        if step:
            z_copies[step - 1].wait_recv()
        level = lax.rem(z + n_z - step, n_z)
        for k in range(1, n_req):
            r_copies[step, k] = send(
                ag2.at[0, 0, level], ag2.at[0, k, level], ss_ag2r.at[step, k],
                rs_ag2r.at[step, k], {"req": r_peer(k)})
    c_copies = [send(ag2.at[0, 0], ag2.at[1, 0], ss_ag2c.at[0], rs_ag2c.at[0], {"mlp": sib})]
    span = n_z * tp

    def unpack(core, k):
        base = (core * n_req + k) * span
        for level in range(n_z):
            xf[base + level * tp:base + (level + 1) * tp, :] = ag2[core, k, level].astype(F32)

    unpack(0, 0)
    for k in range(1, n_req):
        for step in range(n_z):
            r_copies[step, k].wait_recv()
        c_copies.append(send(
            ag2.at[0, k], ag2.at[1, k], ss_ag2c.at[k], rs_ag2c.at[k], {"mlp": sib}))
        unpack(0, k)
    for k, copy in enumerate(c_copies):
        copy.wait_recv()
        unpack(1, k)
    xb[...] = xf[...].astype(BF16)

    loads["g"].wait()
    loads["u"].wait()

    def ffn_hidden(start, size):
        gate = lax.dot_general(
            xb[...], wg[pl.ds(start, size), :], NT, preferred_element_type=F32)
        up = lax.dot_general(
            xb[...], wu[pl.ds(start, size), :], NT, preferred_element_type=F32)
        inner = GELU_C * (gate + 0.044715 * (gate * gate * gate))
        hid[:, pl.ds(start, size)] = (0.5 * gate * (1.0 + jnp.tanh(inner)) * up).astype(BF16)

    if ff >= 256:
        @pl.loop(0, ff // 256)
        def _(step):
            ffn_hidden(pl.multiple_of(step * 256, 256), 256)
    if ff % 256:
        ffn_hidden(ff - ff % 256, ff % 256)
    loads["d"].wait()

    parts, cols = t1.shape[1], t1.shape[-1]
    order = list(range(1, n_req)) + [0]
    first, second, third, kept, finals = {}, {}, {}, {}, {}

    def partial_sums(j):
        @pl.loop(0, cols // 512)
        def _(step):
            start = pl.multiple_of(step * 512, 512)
            acc[j, :, pl.ds(start, 512)] = jnp.dot(
                hid[...], wd[:, pl.ds(j * cols + start, 512)], preferred_element_type=F32)

        for core in (1, 0):
            for k in order:
                base = (core * n_req + k) * span
                for level in range(n_z):
                    row = base + level * tp
                    t1[core, j, k, level] = acc[j, row:row + tp, :].astype(BF16)
                if core:
                    first[j, k] = send(
                        t1.at[1, j, k], u1.at[j, k], ss_t1.at[j, k], rs_t1.at[j, k], {"mlp": sib})

    def add_cores(j):
        for k in order:
            first[j, k].wait_recv()
            both = t1[0, j, k].astype(F32) + u1[j, k].astype(F32)
            if k:
                t2[j, k] = both.astype(BF16)
                second[j, k] = send(
                    t2.at[j, k], u2.at[j, k], ss_t2.at[j, k], rs_t2.at[j, k],
                    {"req": r_peer(n_req - k)})
            else:
                t3f[j] = both

    def add_req(j):
        both = t3f[j]
        for k in range(1, n_req):
            second[j, k].wait_recv()
            both = both + u2[j, k].astype(F32)
        t3f[j] = both
        t3[j] = both.astype(BF16)
        for k in range(1, n_z):
            third[j, k] = send(
                t3.at[j, lax.rem(z + k, n_z)], u3.at[j, k], ss_t3.at[j, k], rs_t3.at[j, k],
                z_peer(k))

    for j in range(parts + 2):
        if j < parts:
            partial_sums(j)
        if 0 <= j - 1 < parts:
            add_cores(j - 1)
        if 0 <= j - 2 < parts:
            add_req(j - 2)
    squares = jnp.zeros((tp, 1), F32)
    for j in range(parts):
        total_j = t3f[j, z]
        for k in range(1, n_z):
            third[j, k].wait_recv()
            total_j = total_j + u3[j, k].astype(F32)
        finals[j] = total_j
        squares = squares + jnp.sum(total_j * total_j, axis=-1, keepdims=True)
    scale = lax.rsqrt(squares / width + EPS)
    for j in range(parts):
        lanes = slice(j * cols, (j + 1) * cols)
        out[:, lanes] = (
            residual[:, lanes] + finals[j] * scale * post_ffn_gain[:, lanes]).astype(BF16)
    for copy in sent:
        copy.wait_send()


def shards(
    n_req, n_mlp,
    tokens, segments, owners, sink_keys, sink_values, window_keys, window_values,
    attn_gain, post_attn_gain, ffn_gain, post_ffn_gain,
    w_query, w_key, w_value, w_out, w_gate, w_up, w_down,
):
    tp, width = tokens.shape
    n_z = n_mlp // 2
    group = tp * n_mlp
    total = group * n_req
    q_cols, kv_cols, ff = w_query.shape[1], w_key.shape[1], w_gate.shape[0]
    extra = 2 * group
    parts = 1
    cols = width // parts
    def v(shape, dtype=BF16):
        return pltpu.VMEM(shape, dtype)

    dma = pltpu.SemaphoreType.DMA
    scratch = [v(a.shape) for a in (
        window_keys, window_values, w_query, w_key, w_value, w_out, w_gate, w_up, w_down)]
    scratch += [v((1, width), F32)] * 4
    scratch += [
        dma((13,)),
        v((total, HD), jnp.int32), v((group, extra), jnp.int32),
        v((2, n_z, tp, width)), v((total, width), F32), v((total, width)),
        v((n_req, group, q_cols)), v((extra, kv_cols), F32), v((extra, kv_cols), F32),
        v((n_req, group, q_cols + HD), F32), v((max(n_req - 1, 1), group, q_cols + HD), F32),
        v((group, width), F32), v((2, n_z, tp, width)), v((n_z, tp, width)),
        v((n_z, tp, width)), v((n_z - 1, tp, width)),
        v((2, n_req, n_z, tp, width)), v((total, ff)), v((parts, total, cols), F32),
        v((2, parts, n_req, n_z, tp, cols)), v((parts, n_req, n_z, tp, cols)),
        v((parts, n_req, n_z, tp, cols)), v((parts, n_req, n_z, tp, cols)),
        v((parts, n_z, tp, cols), F32), v((parts, n_z, tp, cols)), v((parts, n_z, tp, cols)),
        dma((n_z,)), dma((n_z,)), dma((n_z,)), dma((n_z,)),
        dma((n_req,)), dma((n_req,)), dma((n_req,)), dma((n_req,)),
        dma, dma, dma((n_z,)), dma((n_z,)),
        dma((n_z,)), dma((n_z,)), dma((n_z, n_req)), dma((n_z, n_req)),
        dma((n_req,)), dma((n_req,)),
        dma((parts, n_req)), dma((parts, n_req)), dma((parts, n_req)), dma((parts, n_req)),
        dma((parts, n_z)), dma((parts, n_z)),
    ]
    vmem = pl.BlockSpec(memory_space=pltpu.VMEM)
    smem = pl.BlockSpec(memory_space=pltpu.SMEM)
    hbm = pl.BlockSpec(memory_space=pl.ANY)
    return pl.pallas_call(
        functools.partial(kernel, n_req, n_mlp),
        name="layer",
        out_shape=jax.ShapeDtypeStruct((tp, width), BF16),
        in_specs=[vmem, smem, smem, vmem, vmem] + [hbm] * 13,
        out_specs=vmem,
        scratch_shapes=scratch,
        compiler_params=pltpu.CompilerParams(
            collective_id=0, has_side_effects=True, vmem_limit_bytes=62 << 20),
    )(
        tokens, segments, owners, sink_keys, sink_values,
        attn_gain, post_attn_gain, ffn_gain, post_ffn_gain,
        window_keys, window_values, w_query, w_key, w_value, w_out, w_gate, w_up, w_down,
    )


def solution(mesh):
    both = P(("req", "mlp"), None)
    return jax.shard_map(
        functools.partial(shards, mesh.shape["req"], mesh.shape["mlp"]),
        mesh=mesh,
        in_specs=(
            both, P(), P(), P(None, "mlp"), P(None, "mlp"), P("req", "mlp"), P("req", "mlp"),
            P(), P(), P(), P(),
            P(None, "mlp"), P(None, "mlp"), P(None, "mlp"), P("mlp", None), both, both, both,
        ),
        out_specs=both,
        check_vma=False,
    )
```
